32 devices in a mesh: batch: 8 (over z, y), mp: 4 (over x, core).
Axes of the slice: x: 2, y: 2, z: 4, core: 2. Of those that a mesh axis runs over, the one named last changes fastest.
Arguments:
- gate_act: bfloat16 [6144, 14336], P('batch', 'mp'), may hold values from -6 to 6
- up_act: bfloat16 [6144, 14336], P('batch', 'mp'), may hold values from -6 to 6
- upstream: bfloat16 [6144, 8192], P('batch', 'mp'), may hold values from -6 to 6
- kept_index: int32 [8, 8], P('batch'), may hold values from 0 to 31, as said below
- kept_count: int32 [8], P('batch'), may hold values from 1 to 8, as said below
Outputs:
- grad_down: bfloat16 [8192, 14336], P('batch', 'mp')
The draws below stay inside these ranges and needn't reach their ends.
Inputs may be any that keep to these rules, and one draw needn't show every extreme that they name: `kept_index`: each group's row names different candidates; only the first kept_count entries of a row are kept. `kept_count`: the counts sum to 8 * 4 over the groups, and some group keeps exactly 8.
All inputs are finite; a program needn't handle non-finite values.
Results may differ from the reference program's by a relative error of at most 0.0049.
Values may be sent and summed in bfloat16 or wider, within the bound.
A program may use at most 128 MiB of HBM per device.

```python
import math
import jax
import jax.numpy as jnp
from jax import lax

D = 8192
FF_W = 14336
SEQ = 24
CAND = 32
GROUPS = 8
KEEP_MAX = 8
CAP = 4
N_BATCH = 8


def draw_kept_count(key, part):
    first_key, second_key = jax.random.split(jax.random.fold_in(key, 11))
    biggest = jax.random.randint(first_key, (), 0, GROUPS)
    counts = jnp.ones((GROUPS,), jnp.int32).at[biggest].set(KEEP_MAX)
    extra = GROUPS * CAP - KEEP_MAX - (GROUPS - 1)
    places = jnp.arange(GROUPS, dtype=jnp.int32)

    def add_one(step, counts):
        anchor = jax.random.randint(jax.random.fold_in(second_key, step), (), 0, GROUPS)
        distance = jnp.mod(places - anchor, GROUPS)
        score = jnp.where(counts < KEEP_MAX, GROUPS - distance, 0)
        target = jnp.argmax(score)
        return counts + (places == target).astype(jnp.int32)
    return lax.fori_loop(0, extra, add_one, counts)


def draw_kept_index(key, part):
    row_keys = jax.random.split(jax.random.fold_in(key, 23), GROUPS)

    def one_row(row_key):
        return jax.random.permutation(row_key, CAND)[:KEEP_MAX].astype(jnp.int32)
    return jax.vmap(one_row)(row_keys)


def spiked(values, own_key, source, target, blocks, factor):
    owner, partner = [(jnp.arange(values.shape[position]) // (values.shape[position] // blocks)).reshape([-1 if axis == position else 1 for axis in range(values.ndim)]) for position in (source, target)]
    chosen = jax.random.permutation(own_key, blocks)[partner]
    strong = (owner == chosen) | (owner == (partner + blocks // 2) % blocks)
    return jnp.where(strong, factor * values, values)


def levels(own_key, dims, cuts, smallest, largest):
    gain = 1.0
    for dim, shards_of in cuts:
        steps = jax.random.uniform(jax.random.fold_in(jax.random.fold_in(own_key, 6), dim), (shards_of,), jnp.float32, smallest / len(cuts), largest / len(cuts))
        gain = gain * jnp.repeat(jnp.exp(steps), dims[dim] // shards_of).reshape((-1,) + (1,) * (len(dims) - 1 - dim))
    return gain


def bell_draw(own_key, extent, spread, reach, cuts=(), kind=jnp.bfloat16):
    result = jax.random.normal(own_key, extent, jnp.float32) * spread
    if len(cuts) > 0:
        result = levels(own_key, extent, cuts, -0.22, 0.18) * result
    return jnp.clip(result, min=-reach, max=reach).astype(kind)


def heavy_noise(stream_key, shape, spread, bound, cuts, heavy, kind=jnp.bfloat16):
    result = spread * jax.random.normal(stream_key, shape, jnp.float32)
    if cuts:
        result = result * levels(stream_key, shape, cuts, -0.22, 0.18)
    return jnp.clip(spiked(result, jax.random.fold_in(stream_key, 3), *heavy), -bound, bound).astype(kind)


def setup_inputs(seed: int = 0) -> dict:
    arg_keys = jax.random.split(jax.random.key(seed), 6)
    gate_act = bell_draw(arg_keys[0], (N_BATCH * CAND * SEQ, FF_W), 1.0, 6.0, ((0, 8), (1, 4)))
    up_act = bell_draw(arg_keys[1], (N_BATCH * CAND * SEQ, FF_W), 1.0, 6.0, ((0, 8), (1, 4)))
    upstream = heavy_noise(arg_keys[2], (N_BATCH * CAND * SEQ, D), 1.0, 6.0, ((0, 8), (1, 4)), (0, 1, 8, 2.0))
    kept_index = draw_kept_index(jax.random.fold_in(arg_keys[5], 71), 0)
    kept_count = draw_kept_count(jax.random.fold_in(arg_keys[5], 71), 0)
    return dict(gate_act=gate_act, up_act=up_act, upstream=upstream, kept_index=kept_index, kept_count=kept_count)


def reference(gate_act, up_act, upstream, kept_index, kept_count):
    gate_all = gate_act.reshape(N_BATCH, CAND, SEQ, FF_W)
    up_all = up_act.reshape(N_BATCH, CAND, SEQ, FF_W)
    grad_all = upstream.reshape(N_BATCH, CAND, SEQ, D)
    slot_ids = jnp.arange(KEEP_MAX, dtype=jnp.int32)

    def per_group(summed, group_id):
        picked = kept_index[group_id]
        present = slot_ids < kept_count[group_id]
        gate_rows = gate_all[group_id][picked].astype(jnp.float32)
        up_rows = up_all[group_id][picked].astype(jnp.float32)
        hidden = (jax.nn.silu(gate_rows) * up_rows).astype(jnp.bfloat16)
        hidden = jnp.where(present[:, None, None], hidden, jnp.zeros_like(hidden))
        grad_rows = grad_all[group_id][picked]
        term = lax.dot_general(grad_rows.reshape(KEEP_MAX * SEQ, D), hidden.reshape(KEEP_MAX * SEQ, FF_W), (((0,), (0,)), ((), ())), preferred_element_type=jnp.float32)
        return (summed + term, None)
    summed, _ = lax.scan(per_group, jnp.zeros((D, FF_W), jnp.float32), jnp.arange(N_BATCH, dtype=jnp.int32))
    factor = 1.0 / math.sqrt(N_BATCH * CAP * SEQ)
    return (summed * factor).astype(jnp.bfloat16)
```

```python
import functools
import math

import jax
import jax.numpy as jnp
from jax import lax
from jax.experimental import pallas as pl
from jax.experimental.pallas import tpu as pltpu
from jax.sharding import PartitionSpec as P

SEQ = 24
CAND = 32
MESH = pl.DeviceIdType.MESH
LEAD = 2


def pick_kernel(index_ref, gate_ref, up_ref, up_grad_ref, hidden_ref, grad_ref):
    gate = gate_ref[...].astype(jnp.float32)
    hidden_ref[...] = (jax.nn.silu(gate) * up_ref[...].astype(jnp.float32)).astype(jnp.bfloat16)
    grad_ref[...] = up_grad_ref[...]


def pick(picked, gate_all, up_all, grad_all):
    keep_most = picked.shape[0]

    def block(width):
        return pl.BlockSpec((1, SEQ, width), lambda j, index: (index[j], 0, 0))

    def out_block(width):
        return pl.BlockSpec((1, SEQ, width), lambda j, index: (j, 0, 0))

    wide, part = gate_all.shape[2], grad_all.shape[2]
    return pl.pallas_call(
        pick_kernel,
        grid_spec=pltpu.PrefetchScalarGridSpec(
            num_scalar_prefetch=1,
            grid=(keep_most,),
            in_specs=[block(wide), block(wide), block(part)],
            out_specs=[out_block(wide), out_block(part)],
        ),
        out_shape=[
            jax.ShapeDtypeStruct((keep_most, SEQ, wide), jnp.bfloat16),
            jax.ShapeDtypeStruct((keep_most, SEQ, part), jnp.bfloat16),
        ],
    )(picked, gate_all, up_all, grad_all)


def exchange_kernel(
    groups, parts, keep_most, total,
    starts_ref, hid_ref, grad_ref, out_ref, gout_ref,
    y_send, y_recv, loc, dn_recv, dn_send, up_recv, up_send, ga, gb, gc,
    ys_sem, yr_sem, dns_sem, dnr_sem, ups_sem, upr_sem, fs_sem, fr_sem,
    as_sem, ar_sem, bs_sem, br_sem, cs_sem, cr_sem, l_sem,
):
    b, m = lax.axis_index("batch"), lax.axis_index("mp")
    planes, pairs = groups // 2, total // 2
    z, y = b // 2, lax.rem(b, 2)
    peer = z * 2 + 1 - y
    ks = keep_most // parts
    ratio = groups // parts
    block = grad_ref.shape[2] // ratio

    def low(plane):
        return jnp.maximum(2 * plane, total - 2 * keep_most * (planes - plane)) // 2

    def high(plane):
        return (jnp.minimum(2 * keep_most * plane, total - 2 * (planes - plane)) + 1) // 2

    barrier = pltpu.get_barrier_semaphore()
    for d in range(1, groups):
        pl.semaphore_signal(barrier, inc=1, device_id=(lax.rem(b + d, groups), m), device_id_type=MESH)
    for d in range(1, parts):
        pl.semaphore_signal(barrier, inc=1, device_id=(b, lax.rem(m + d, parts)), device_id_type=MESH)
    pl.semaphore_wait(barrier, groups + parts - 2)

    def copy_a(d):
        other = lax.rem(m + d, parts)
        return pltpu.make_async_remote_copy(
            src_ref=grad_ref.at[pl.ds(other * ks, ks)], dst_ref=ga.at[m],
            send_sem=as_sem.at[d], recv_sem=ar_sem.at[d],
            device_id=(b, other), device_id_type=MESH)

    def copy_b(d):
        other = lax.rem(b + d, groups)
        return pltpu.make_async_remote_copy(
            src_ref=ga.at[other // ratio, :, :, pl.ds(pl.multiple_of(lax.rem(other, ratio) * block, block), block)],
            dst_ref=gb.at[b],
            send_sem=bs_sem.at[d], recv_sem=br_sem.at[d],
            device_id=(other, m), device_id_type=MESH)

    def copy_c(d):
        other = lax.rem(m + d, parts)
        return pltpu.make_async_remote_copy(
            src_ref=gb, dst_ref=gc.at[m],
            send_sem=cs_sem.at[d], recv_sem=cr_sem.at[d],
            device_id=(b, other), device_id_type=MESH)

    def copy_y(k):
        return pltpu.make_async_remote_copy(
            src_ref=y_send.at[k], dst_ref=y_recv.at[k],
            send_sem=ys_sem.at[k], recv_sem=yr_sem.at[k],
            device_id=(peer, m), device_id_type=MESH)

    def copy_dn(p):
        return pltpu.make_async_remote_copy(
            src_ref=dn_send.at[p], dst_ref=dn_recv.at[p],
            send_sem=dns_sem.at[p], recv_sem=dnr_sem.at[p],
            device_id=(lax.rem(b + groups - 2, groups), m), device_id_type=MESH)

    def copy_up(p):
        return pltpu.make_async_remote_copy(
            src_ref=up_send.at[p], dst_ref=up_recv.at[p],
            send_sem=ups_sem.at[p], recv_sem=upr_sem.at[p],
            device_id=(lax.rem(b + 2, groups), m), device_id_type=MESH)

    def copy_f(p):
        return pltpu.make_async_remote_copy(
            src_ref=out_ref.at[p, y], dst_ref=out_ref.at[p, y],
            send_sem=fs_sem.at[p], recv_sem=fr_sem.at[p],
            device_id=(peer, m), device_id_type=MESH)

    for d in range(1, parts):
        copy_a(d).start()

    my_start, peer_start = starts_ref[b], starts_ref[peer]
    offset = lax.rem(1 - y + my_start, 2)

    @pl.loop(0, keep_most // 2)
    def _(k):
        y_send[k] = hid_ref[2 * k + offset]
        copy_y(k).start()

    own = pltpu.make_async_copy(grad_ref.at[pl.ds(m * ks, ks)], ga.at[m], l_sem.at[0])
    own.start()
    own.wait()
    for d in range(1, parts):
        copy_a(d).wait()
    for d in range(1, groups):
        copy_b(d).start()
    own = pltpu.make_async_copy(
        ga.at[b // ratio, :, :, pl.ds(pl.multiple_of(lax.rem(b, ratio) * block, block), block)], gb.at[b], l_sem.at[1])
    own.start()
    own.wait()

    @pl.loop(0, keep_most // 2)
    def _(k):
        copy_y(k).wait()

    plane_start = starts_ref[2 * z]
    plane_end = starts_ref[2 * z + 2]
    my_end = starts_ref[b + 1]

    @pl.loop(0, pairs)
    def _(p):
        number = 2 * p + y
        mine = hid_ref[jnp.clip(number - my_start, 0, keep_most - 1)]
        theirs = y_recv[jnp.clip((number - peer_start) // 2, 0, keep_most // 2 - 1)]
        is_mine = jnp.logical_and(number >= my_start, number < my_end)
        loc[p] = jnp.where(is_mine, mine, theirs)

    def gets_dn(p):
        return jnp.logical_and(z < planes - 1, p >= low(z + 1))

    def gets_up(p):
        return jnp.logical_and(z > 0, p < high(z))

    @pl.loop(0, pairs + LEAD * planes)
    def _(t):
        pd = t - LEAD * (planes - 1 - z)
        pu = t - LEAD * z
        pf = t - LEAD * planes

        @pl.when(jnp.logical_and(pd >= 0, pd < pairs))
        def _():
            @pl.when(gets_dn(pd))
            def _():
                copy_dn(pd).wait_recv()

                @pl.when(z > 0)
                def _():
                    dn_send[pd] = jnp.where(2 * pd + y >= plane_end, dn_recv[pd], loc[pd])
                    copy_dn(pd).start()

            @pl.when(jnp.logical_and(jnp.logical_not(gets_dn(pd)), jnp.logical_and(z > 0, pd >= low(z))))
            def _():
                dn_send[pd] = loc[pd]
                copy_dn(pd).start()

        @pl.when(jnp.logical_and(pu >= 0, pu < pairs))
        def _():
            @pl.when(gets_up(pu))
            def _():
                copy_up(pu).wait_recv()

                @pl.when(z < planes - 1)
                def _():
                    up_send[pu] = jnp.where(2 * pu + y < plane_start, up_recv[pu], loc[pu])
                    copy_up(pu).start()

            @pl.when(jnp.logical_and(jnp.logical_not(gets_up(pu)), jnp.logical_and(z < planes - 1, pu < high(z + 1))))
            def _():
                up_send[pu] = loc[pu]
                copy_up(pu).start()

        @pl.when(pf >= 0)
        def _():
            number = 2 * pf + y
            out_ref[pf, y] = loc[pf]

            @pl.when(gets_dn(pf))
            def _():
                out_ref[pf, y] = jnp.where(number >= plane_end, dn_recv[pf], out_ref[pf, y])

            @pl.when(gets_up(pf))
            def _():
                out_ref[pf, y] = jnp.where(number < plane_start, up_recv[pf], out_ref[pf, y])

            copy_f(pf).start()

    for d in range(1, groups):
        copy_b(d).wait()
    for d in range(1, parts):
        copy_c(d).start()
    own = pltpu.make_async_copy(gb, gc.at[m], l_sem.at[2])
    own.start()
    own.wait()
    for d in range(1, parts):
        copy_c(d).wait()

    @pl.loop(0, total)
    def _(i):
        g = jnp.int32(0)
        for q in range(1, groups):
            g = g + (starts_ref[q] <= i).astype(jnp.int32)
        j = jnp.clip(i - starts_ref[g], 0, keep_most - 1)
        gout_ref[i] = gc[j // ks, g, lax.rem(j, ks)]

    @pl.loop(0, pairs)
    def _(p):
        copy_f(p).wait_send()
        pltpu.make_async_remote_copy(
            src_ref=out_ref.at[p, 1 - y], dst_ref=out_ref.at[p, 1 - y],
            send_sem=fs_sem.at[p], recv_sem=fr_sem.at[p],
            device_id=(peer, m), device_id_type=MESH).wait_recv()

        @pl.when(jnp.logical_and(z > 0, p >= low(z)))
        def _():
            copy_dn(p).wait_send()

        @pl.when(jnp.logical_and(z < planes - 1, p < high(z + 1)))
        def _():
            copy_up(p).wait_send()


def exchange(starts, hid, grad, groups, parts, total):
    keep_most, _, wide = hid.shape
    part = grad.shape[2]
    pairs = total // 2
    ks = keep_most // parts
    block = part * parts // groups
    bf16 = jnp.bfloat16
    dma = pltpu.SemaphoreType.DMA
    chain = pltpu.VMEM((pairs, SEQ, wide), bf16)
    return pl.pallas_call(
        functools.partial(exchange_kernel, groups, parts, keep_most, total),
        out_shape=[
            jax.ShapeDtypeStruct((pairs, 2, SEQ, wide), bf16),
            jax.ShapeDtypeStruct((total, SEQ, block), bf16),
        ],
        in_specs=[
            pl.BlockSpec(memory_space=pltpu.SMEM),
            pl.BlockSpec(memory_space=pltpu.VMEM),
            pl.BlockSpec(memory_space=pltpu.VMEM),
        ],
        out_specs=[pl.BlockSpec(memory_space=pltpu.VMEM)] * 2,
        scratch_shapes=[
            pltpu.VMEM((keep_most // 2, SEQ, wide), bf16),
            pltpu.VMEM((keep_most // 2, SEQ, wide), bf16),
            chain, chain, chain, chain, chain,
            pltpu.VMEM((parts, ks, SEQ, part), bf16),
            pltpu.VMEM((groups, ks, SEQ, block), bf16),
            pltpu.VMEM((parts, groups, ks, SEQ, block), bf16),
            dma((keep_most // 2,)), dma((keep_most // 2,)),
            dma((pairs,)), dma((pairs,)), dma((pairs,)), dma((pairs,)), dma((pairs,)), dma((pairs,)),
            dma((parts,)), dma((parts,)), dma((groups,)), dma((groups,)), dma((parts,)), dma((parts,)),
            dma((3,)),
        ],
        compiler_params=pltpu.CompilerParams(
            collective_id=0, has_side_effects=True, vmem_limit_bytes=60 * 1024 * 1024
        ),
    )(starts, hid, grad)


def on_device(gate_act, up_act, upstream, kept_index, kept_count):
    groups, parts = lax.axis_size("batch"), lax.axis_size("mp")
    share = groups // 2
    total = groups * share
    wide, part = gate_act.shape[1], upstream.shape[1]
    hid, grad = pick(
        kept_index[0],
        gate_act.reshape(CAND, SEQ, wide),
        up_act.reshape(CAND, SEQ, wide),
        upstream.reshape(CAND, SEQ, part),
    )
    counts = lax.all_gather(kept_count, "batch", axis=0, tiled=True)
    starts = jnp.concatenate([jnp.zeros((1,), jnp.int32), jnp.cumsum(counts)])
    rows, columns = exchange(starts, hid, grad, groups, parts, total)
    summed = lax.dot_general(
        columns.reshape(total * SEQ, columns.shape[2]),
        rows.reshape(total * SEQ, wide),
        (((0,), (0,)), ((), ())),
        preferred_element_type=jnp.float32,
    )
    return (summed * (1.0 / math.sqrt(total * SEQ))).astype(jnp.bfloat16)


def solution(mesh):
    placed = (P("batch", "mp"), P("batch", "mp"), P("batch", "mp"), P("batch", None), P("batch"))
    return jax.shard_map(
        on_device, mesh=mesh, in_specs=placed, out_specs=P("batch", "mp"), check_vma=False
    )
```

```python
import functools
import math

import jax
import jax.numpy as jnp
from jax import lax
from jax.experimental import pallas as pl
from jax.experimental.pallas import tpu as pltpu
from jax.sharding import PartitionSpec as P

SEQ = 24
CAND = 32
MESH = pl.DeviceIdType.MESH
LEAD = 3


def pick_kernel(index_ref, gate_ref, up_ref, up_grad_ref, hidden_ref, grad_ref):
    gate = gate_ref[...].astype(jnp.float32)
    hidden_ref[...] = (jax.nn.silu(gate) * up_ref[...].astype(jnp.float32)).astype(jnp.bfloat16)
    grad_ref[...] = up_grad_ref[...]


def pick(picked, gate_all, up_all, grad_all):
    keep_most = picked.shape[0]

    def block(width):
        return pl.BlockSpec((1, SEQ, width), lambda j, index: (index[j], 0, 0))

    def out_block(width):
        return pl.BlockSpec((1, SEQ, width), lambda j, index: (j, 0, 0))

    wide, part = gate_all.shape[2], grad_all.shape[2]
    return pl.pallas_call(
        pick_kernel,
        grid_spec=pltpu.PrefetchScalarGridSpec(
            num_scalar_prefetch=1,
            grid=(keep_most,),
            in_specs=[block(wide), block(wide), block(part)],
            out_specs=[out_block(wide), out_block(part)],
        ),
        out_shape=[
            jax.ShapeDtypeStruct((keep_most, SEQ, wide), jnp.bfloat16),
            jax.ShapeDtypeStruct((keep_most, SEQ, part), jnp.bfloat16),
        ],
    )(picked, gate_all, up_all, grad_all)


def exchange_kernel(
    groups, parts, keep_most, total, chunks,
    count_ref, hid_ref, grad_ref, out_ref, gout_ref,
    counts_in, counts_ref, starts_ref,
    y_send, y_recv, loc, dn_recv, dn_send, up_recv, up_send, ga, gb, gc,
    ys_sem, yr_sem, dns_sem, dnr_sem, ups_sem, upr_sem, fs_sem, fr_sem,
    as_sem, ar_sem, bs_sem, br_sem, cs_sem, cr_sem, ns_sem, nr_sem, l_sem,
):
    b, m = lax.axis_index("batch"), lax.axis_index("mp")
    planes, pairs = groups // 2, total // 2
    z, y = b // 2, lax.rem(b, 2)
    peer = z * 2 + 1 - y
    ks = keep_most // parts
    ratio = groups // parts
    block = grad_ref.shape[2] // ratio
    width = hid_ref.shape[2] // chunks
    half = keep_most // 2
    steps = chunks * pairs

    def cols(c):
        if isinstance(c, int):
            return pl.ds(c * width, width)
        return pl.ds(pl.multiple_of(c * width, width), width)

    def low(plane):
        return jnp.maximum(2 * plane, total - 2 * keep_most * (planes - plane)) // 2

    def high(plane):
        return (jnp.minimum(2 * keep_most * plane, total - 2 * (planes - plane)) + 1) // 2

    barrier = pltpu.get_barrier_semaphore()
    for d in range(1, groups):
        pl.semaphore_signal(barrier, inc=1, device_id=(lax.rem(b + d, groups), m), device_id_type=MESH)
    for d in range(1, parts):
        pl.semaphore_signal(barrier, inc=1, device_id=(b, lax.rem(m + d, parts)), device_id_type=MESH)
    pl.semaphore_wait(barrier, groups + parts - 2)

    def copy_a(d):
        other = lax.rem(m + d, parts)
        return pltpu.make_async_remote_copy(
            src_ref=grad_ref.at[pl.ds(other * ks, ks)], dst_ref=ga.at[m],
            send_sem=as_sem.at[d], recv_sem=ar_sem.at[d],
            device_id=(b, other), device_id_type=MESH)

    def copy_b(d):
        other = lax.rem(b + d, groups)
        return pltpu.make_async_remote_copy(
            src_ref=ga.at[other // ratio, :, :, pl.ds(pl.multiple_of(lax.rem(other, ratio) * block, block), block)],
            dst_ref=gb.at[b],
            send_sem=bs_sem.at[d], recv_sem=br_sem.at[d],
            device_id=(other, m), device_id_type=MESH)

    def copy_c(d):
        other = lax.rem(m + d, parts)
        return pltpu.make_async_remote_copy(
            src_ref=gb, dst_ref=gc.at[m],
            send_sem=cs_sem.at[d], recv_sem=cr_sem.at[d],
            device_id=(b, other), device_id_type=MESH)

    def copy_n(d):
        return pltpu.make_async_remote_copy(
            src_ref=count_ref, dst_ref=counts_in.at[b],
            send_sem=ns_sem.at[d], recv_sem=nr_sem.at[d],
            device_id=(lax.rem(b + d, groups), m), device_id_type=MESH)

    def copy_y(c, k):
        return pltpu.make_async_remote_copy(
            src_ref=y_send.at[k, :, cols(c)], dst_ref=y_recv[c].at[k],
            send_sem=ys_sem.at[c * half + k], recv_sem=yr_sem.at[c * half + k],
            device_id=(peer, m), device_id_type=MESH)

    def copy_dn(s):
        p, c = lax.rem(s, pairs), s // pairs
        return pltpu.make_async_remote_copy(
            src_ref=dn_send.at[p, :, cols(c)], dst_ref=dn_recv.at[p, :, cols(c)],
            send_sem=dns_sem.at[s], recv_sem=dnr_sem.at[s],
            device_id=(lax.rem(b + groups - 2, groups), m), device_id_type=MESH)

    def copy_up(s):
        p, c = lax.rem(s, pairs), s // pairs
        return pltpu.make_async_remote_copy(
            src_ref=up_send.at[p, :, cols(c)], dst_ref=up_recv.at[p, :, cols(c)],
            send_sem=ups_sem.at[s], recv_sem=upr_sem.at[s],
            device_id=(lax.rem(b + 2, groups), m), device_id_type=MESH)

    def copy_f(s, side):
        p, c = lax.rem(s, pairs), s // pairs
        return pltpu.make_async_remote_copy(
            src_ref=out_ref.at[p, side, :, cols(c)], dst_ref=out_ref.at[p, side, :, cols(c)],
            send_sem=fs_sem.at[s], recv_sem=fr_sem.at[s],
            device_id=(peer, m), device_id_type=MESH)

    for d in range(1, groups):
        copy_n(d).start()
    own = pltpu.make_async_copy(count_ref, counts_in.at[b], l_sem.at[3])
    own.start()
    for d in range(1, parts):
        copy_a(d).start()

    own.wait()
    for d in range(1, groups):
        copy_n(d).wait()
    to_scalars = pltpu.make_async_copy(counts_in, counts_ref, l_sem.at[4])
    to_scalars.start()
    to_scalars.wait()
    before = jnp.int32(0)
    for g in range(groups):
        starts_ref[g] = before
        before = before + counts_ref[g, 0, 0]
    starts_ref[groups] = before

    my_start, peer_start = starts_ref[b], starts_ref[peer]
    offset = lax.rem(1 - y + my_start, 2)

    @pl.loop(0, half)
    def _(k):
        y_send[k] = hid_ref[2 * k + offset]
        copy_y(0, k).start()

    for c in range(1, chunks):

        @pl.loop(0, half)
        def _(k):
            copy_y(c, k).start()

    own = pltpu.make_async_copy(grad_ref.at[pl.ds(m * ks, ks)], ga.at[m], l_sem.at[0])
    own.start()
    own.wait()
    for d in range(1, parts):
        copy_a(d).wait()
    for d in range(1, groups):
        copy_b(d).start()
    own = pltpu.make_async_copy(
        ga.at[b // ratio, :, :, pl.ds(pl.multiple_of(lax.rem(b, ratio) * block, block), block)], gb.at[b], l_sem.at[1])
    own.start()
    own.wait()

    plane_start = starts_ref[2 * z]
    plane_end = starts_ref[2 * z + 2]
    my_end = starts_ref[b + 1]
    far = jnp.maximum(z, planes - 1 - z)

    def place(s, c):
        p = lax.rem(s, pairs)
        number = 2 * p + y
        mine = hid_ref[jnp.clip(number - my_start, 0, keep_most - 1), :, cols(c)]
        theirs = y_recv[c][jnp.clip((number - peer_start) // 2, 0, half - 1)]
        is_mine = jnp.logical_and(number >= my_start, number < my_end)
        loc[p, :, cols(c)] = jnp.where(is_mine, mine, theirs)

    def gets_dn(s):
        return jnp.logical_and(z < planes - 1, lax.rem(s, pairs) >= low(z + 1))

    def gets_up(s):
        return jnp.logical_and(z > 0, lax.rem(s, pairs) < high(z))

    def gives_dn(s):
        return jnp.logical_and(z > 0, lax.rem(s, pairs) >= low(z))

    def gives_up(s):
        return jnp.logical_and(z < planes - 1, lax.rem(s, pairs) < high(z + 1))

    @pl.loop(0, steps + LEAD * (planes - 1))
    def _(t):
        sd = t - LEAD * (planes - 1 - z)
        su = t - LEAD * z
        sf = t - LEAD * far

        for c in range(chunks):

            @pl.when(t == c * pairs)
            def _():
                @pl.loop(0, half)
                def _(k):
                    copy_y(c, k).wait()

            @pl.when(jnp.logical_and(t >= c * pairs, t < (c + 1) * pairs))
            def _():
                place(t, c)

        @pl.when(t == steps // 3)
        def _():
            for d in range(1, groups):
                copy_b(d).wait()
            for d in range(1, parts):
                copy_c(d).start()

        @pl.when(jnp.logical_and(sd >= 0, sd < steps))
        def _():
            p, c = lax.rem(sd, pairs), sd // pairs

            @pl.when(gets_dn(sd))
            def _():
                copy_dn(sd).wait_recv()

                @pl.when(z > 0)
                def _():
                    dn_send[p, :, cols(c)] = jnp.where(
                        2 * p + y >= plane_end, dn_recv[p, :, cols(c)], loc[p, :, cols(c)])
                    copy_dn(sd).start()

            @pl.when(jnp.logical_and(jnp.logical_not(gets_dn(sd)), gives_dn(sd)))
            def _():
                dn_send[p, :, cols(c)] = loc[p, :, cols(c)]
                copy_dn(sd).start()

        @pl.when(jnp.logical_and(su >= 0, su < steps))
        def _():
            p, c = lax.rem(su, pairs), su // pairs

            @pl.when(gets_up(su))
            def _():
                copy_up(su).wait_recv()

                @pl.when(z < planes - 1)
                def _():
                    up_send[p, :, cols(c)] = jnp.where(
                        2 * p + y < plane_start, up_recv[p, :, cols(c)], loc[p, :, cols(c)])
                    copy_up(su).start()

            @pl.when(jnp.logical_and(jnp.logical_not(gets_up(su)), gives_up(su)))
            def _():
                up_send[p, :, cols(c)] = loc[p, :, cols(c)]
                copy_up(su).start()

        @pl.when(jnp.logical_and(sf >= 0, sf < steps))
        def _():
            p, c = lax.rem(sf, pairs), sf // pairs
            number = 2 * p + y
            out_ref[p, y, :, cols(c)] = loc[p, :, cols(c)]

            @pl.when(gets_dn(sf))
            def _():
                out_ref[p, y, :, cols(c)] = jnp.where(
                    number >= plane_end, dn_recv[p, :, cols(c)], out_ref[p, y, :, cols(c)])

            @pl.when(gets_up(sf))
            def _():
                out_ref[p, y, :, cols(c)] = jnp.where(
                    number < plane_start, up_recv[p, :, cols(c)], out_ref[p, y, :, cols(c)])

            copy_f(sf, y).start()

    own = pltpu.make_async_copy(gb, gc.at[m], l_sem.at[2])
    own.start()
    own.wait()
    for d in range(1, parts):
        copy_c(d).wait()

    @pl.loop(0, total)
    def _(i):
        g = jnp.int32(0)
        for q in range(1, groups):
            g = g + (starts_ref[q] <= i).astype(jnp.int32)
        j = jnp.clip(i - starts_ref[g], 0, keep_most - 1)
        gout_ref[i] = gc[j // ks, g, lax.rem(j, ks)]

    @pl.loop(0, steps)
    def _(s):
        copy_f(s, y).wait_send()
        copy_f(s, 1 - y).wait_recv()

        @pl.when(gives_dn(s))
        def _():
            copy_dn(s).wait_send()

        @pl.when(gives_up(s))
        def _():
            copy_up(s).wait_send()


def exchange(count, hid, grad, groups, parts, total):
    keep_most, _, wide = hid.shape
    part = grad.shape[2]
    pairs = total // 2
    ks = keep_most // parts
    block = part * parts // groups
    bf16 = jnp.bfloat16
    chunks = 2 if wide % 256 == 0 else 1
    steps = chunks * pairs
    count = jnp.broadcast_to(count.reshape(1, 1), (1, 128))
    dma = pltpu.SemaphoreType.DMA
    chain = pltpu.VMEM((pairs, SEQ, wide), bf16)
    return pl.pallas_call(
        functools.partial(exchange_kernel, groups, parts, keep_most, total, chunks),
        out_shape=[
            jax.ShapeDtypeStruct((pairs, 2, SEQ, wide), bf16),
            jax.ShapeDtypeStruct((total, SEQ, block), bf16),
        ],
        in_specs=[
            pl.BlockSpec(memory_space=pltpu.VMEM),
            pl.BlockSpec(memory_space=pltpu.VMEM),
            pl.BlockSpec(memory_space=pltpu.VMEM),
        ],
        out_specs=[pl.BlockSpec(memory_space=pltpu.VMEM)] * 2,
        scratch_shapes=[
            pltpu.VMEM((groups, 1, 128), jnp.int32),
            pltpu.SMEM((groups, 1, 128), jnp.int32),
            pltpu.SMEM((groups + 1,), jnp.int32),
            pltpu.VMEM((keep_most // 2, SEQ, wide), bf16),
            [pltpu.VMEM((keep_most // 2, SEQ, wide // chunks), bf16)] * chunks,
            chain, chain, chain, chain, chain,
            pltpu.VMEM((parts, ks, SEQ, part), bf16),
            pltpu.VMEM((groups, ks, SEQ, block), bf16),
            pltpu.VMEM((parts, groups, ks, SEQ, block), bf16),
            dma((chunks * keep_most // 2,)), dma((chunks * keep_most // 2,)),
            dma((steps,)), dma((steps,)), dma((steps,)), dma((steps,)), dma((steps,)), dma((steps,)),
            dma((parts,)), dma((parts,)), dma((groups,)), dma((groups,)), dma((parts,)), dma((parts,)),
            dma((groups,)), dma((groups,)), dma((5,)),
        ],
        compiler_params=pltpu.CompilerParams(
            collective_id=0, has_side_effects=True, vmem_limit_bytes=60 * 1024 * 1024
        ),
    )(count, hid, grad)


def on_device(gate_act, up_act, upstream, kept_index, kept_count):
    groups, parts = lax.axis_size("batch"), lax.axis_size("mp")
    share = groups // 2
    total = groups * share
    wide, part = gate_act.shape[1], upstream.shape[1]
    hid, grad = pick(
        kept_index[0],
        gate_act.reshape(CAND, SEQ, wide),
        up_act.reshape(CAND, SEQ, wide),
        upstream.reshape(CAND, SEQ, part),
    )
    rows, columns = exchange(kept_count, hid, grad, groups, parts, total)
    summed = lax.dot_general(
        columns.reshape(total * SEQ, columns.shape[2]),
        rows.reshape(total * SEQ, wide),
        (((0,), (0,)), ((), ())),
        preferred_element_type=jnp.float32,
    )
    return (summed * (1.0 / math.sqrt(total * SEQ))).astype(jnp.bfloat16)


def solution(mesh):
    placed = (P("batch", "mp"), P("batch", "mp"), P("batch", "mp"), P("batch", None), P("batch"))
    return jax.shard_map(
        on_device, mesh=mesh, in_specs=placed, out_specs=P("batch", "mp"), check_vma=False
    )
```

```python
import functools
import math

import jax
import jax.numpy as jnp
from jax import lax
from jax.experimental import pallas as pl
from jax.experimental.pallas import tpu as pltpu
from jax.sharding import PartitionSpec as P

SEQ = 24
CAND = 32
MESH = pl.DeviceIdType.MESH
LEAD = 4


def pick_kernel(keep_most, index_ref, gate_all, up_all, grad_all, hidden_ref, grad_ref, gate, up, sems):
    def copies(j):
        at = index_ref[j]
        return (
            pltpu.make_async_copy(gate_all.at[at], gate.at[j], sems.at[0, j]),
            pltpu.make_async_copy(up_all.at[at], up.at[j], sems.at[1, j]),
            pltpu.make_async_copy(grad_all.at[at], grad_ref.at[j], sems.at[2, j]),
        )

    for j in range(keep_most):
        for copy in copies(j)[:2]:
            copy.start()
    for j in range(keep_most):
        copies(j)[2].start()

    @pl.loop(0, keep_most)
    def _(j):
        for copy in copies(j)[:2]:
            copy.wait()
        v = gate[j].astype(jnp.float32)
        hidden_ref[j] = (jax.nn.silu(v) * up[j].astype(jnp.float32)).astype(jnp.bfloat16)

    for j in range(keep_most):
        copies(j)[2].wait()


def pick(picked, gate_all, up_all, grad_all):
    keep_most = picked.shape[0]
    wide, part = gate_all.shape[2], grad_all.shape[2]
    rows = pltpu.VMEM((keep_most, SEQ, wide), jnp.bfloat16)
    return pl.pallas_call(
        functools.partial(pick_kernel, keep_most),
        in_specs=[pl.BlockSpec(memory_space=pltpu.SMEM)] + [pl.BlockSpec(memory_space=pl.ANY)] * 3,
        out_specs=[pl.BlockSpec(memory_space=pltpu.VMEM)] * 2,
        out_shape=[
            jax.ShapeDtypeStruct((keep_most, SEQ, wide), jnp.bfloat16),
            jax.ShapeDtypeStruct((keep_most, SEQ, part), jnp.bfloat16),
        ],
        scratch_shapes=[rows, rows, pltpu.SemaphoreType.DMA((3, keep_most))],
    )(picked, gate_all, up_all, grad_all)


def exchange_kernel(
    groups, parts, keep_most, total, chunks,
    count_ref, hid_ref, grad_ref, out_ref, gout_ref,
    counts_in, counts_ref, starts_ref,
    y_send, y_recv, loc, dn_recv, dn_send, up_recv, up_send, ga, gb, gc,
    ys_sem, yr_sem, dns_sem, dnr_sem, ups_sem, upr_sem, fs_sem, fr_sem,
    as_sem, ar_sem, bs_sem, br_sem, cs_sem, cr_sem, ns_sem, nr_sem, l_sem,
):
    b, m = lax.axis_index("batch"), lax.axis_index("mp")
    planes, pairs = groups // 2, total // 2
    z, y = b // 2, lax.rem(b, 2)
    peer = z * 2 + 1 - y
    ks = keep_most // parts
    ratio = groups // parts
    block = grad_ref.shape[2] // ratio
    width = hid_ref.shape[2] // chunks
    half = keep_most // 2
    steps = chunks * pairs

    def cols(c):
        if isinstance(c, int):
            return pl.ds(c * width, width)
        return pl.ds(pl.multiple_of(c * width, width), width)

    def low(plane):
        return jnp.maximum(2 * plane, total - 2 * keep_most * (planes - plane)) // 2

    def high(plane):
        return (jnp.minimum(2 * keep_most * plane, total - 2 * (planes - plane)) + 1) // 2

    barrier = pltpu.get_barrier_semaphore()
    for d in range(1, groups):
        pl.semaphore_signal(barrier, inc=1, device_id=(lax.rem(b + d, groups), m), device_id_type=MESH)
    for d in range(1, parts):
        pl.semaphore_signal(barrier, inc=1, device_id=(b, lax.rem(m + d, parts)), device_id_type=MESH)
    pl.semaphore_wait(barrier, groups + parts - 2)

    def copy_a(d):
        other = lax.rem(m + d, parts)
        return pltpu.make_async_remote_copy(
            src_ref=grad_ref.at[pl.ds(other * ks, ks)], dst_ref=ga.at[m],
            send_sem=as_sem.at[d], recv_sem=ar_sem.at[d],
            device_id=(b, other), device_id_type=MESH)

    def copy_b(d):
        other = lax.rem(b + d, groups)
        return pltpu.make_async_remote_copy(
            src_ref=ga.at[other // ratio, :, :, pl.ds(pl.multiple_of(lax.rem(other, ratio) * block, block), block)],
            dst_ref=gb.at[b],
            send_sem=bs_sem.at[d], recv_sem=br_sem.at[d],
            device_id=(other, m), device_id_type=MESH)

    def copy_c(d):
        other = lax.rem(m + d, parts)
        return pltpu.make_async_remote_copy(
            src_ref=gb, dst_ref=gc.at[m],
            send_sem=cs_sem.at[d], recv_sem=cr_sem.at[d],
            device_id=(b, other), device_id_type=MESH)

    def copy_n(d):
        return pltpu.make_async_remote_copy(
            src_ref=count_ref, dst_ref=counts_in.at[b],
            send_sem=ns_sem.at[d], recv_sem=nr_sem.at[d],
            device_id=(lax.rem(b + d, groups), m), device_id_type=MESH)

    def copy_y(c, k):
        return pltpu.make_async_remote_copy(
            src_ref=y_send.at[k, :, cols(c)], dst_ref=y_recv[c].at[k],
            send_sem=ys_sem.at[c * half + k], recv_sem=yr_sem.at[c * half + k],
            device_id=(peer, m), device_id_type=MESH)

    def copy_dn(s):
        p, c = lax.rem(s, pairs), s // pairs
        return pltpu.make_async_remote_copy(
            src_ref=dn_send.at[p, :, cols(c)], dst_ref=dn_recv.at[p, :, cols(c)],
            send_sem=dns_sem.at[s], recv_sem=dnr_sem.at[s],
            device_id=(lax.rem(b + groups - 2, groups), m), device_id_type=MESH)

    def copy_up(s):
        p, c = lax.rem(s, pairs), s // pairs
        return pltpu.make_async_remote_copy(
            src_ref=up_send.at[p, :, cols(c)], dst_ref=up_recv.at[p, :, cols(c)],
            send_sem=ups_sem.at[s], recv_sem=upr_sem.at[s],
            device_id=(lax.rem(b + 2, groups), m), device_id_type=MESH)

    def copy_f(s, side):
        p, c = lax.rem(s, pairs), s // pairs
        return pltpu.make_async_remote_copy(
            src_ref=out_ref.at[p, side, :, cols(c)], dst_ref=out_ref.at[p, side, :, cols(c)],
            send_sem=fs_sem.at[s], recv_sem=fr_sem.at[s],
            device_id=(peer, m), device_id_type=MESH)

    for d in range(1, groups):
        copy_n(d).start()
    own = pltpu.make_async_copy(count_ref, counts_in.at[b], l_sem.at[3])
    own.start()
    for d in range(1, parts):
        copy_a(d).start()

    own.wait()
    for d in range(1, groups):
        copy_n(d).wait()
    to_scalars = pltpu.make_async_copy(counts_in, counts_ref, l_sem.at[4])
    to_scalars.start()
    to_scalars.wait()
    before = jnp.int32(0)
    for g in range(groups):
        starts_ref[g] = before
        before = before + counts_ref[g, 0, 0]
    starts_ref[groups] = before

    my_start, peer_start = starts_ref[b], starts_ref[peer]
    offset = lax.rem(1 - y + my_start, 2)

    @pl.loop(0, half)
    def _(k):
        y_send[k] = hid_ref[2 * k + offset]
        copy_y(0, k).start()

    for c in range(1, chunks):

        @pl.loop(0, half)
        def _(k):
            copy_y(c, k).start()

    own = pltpu.make_async_copy(grad_ref.at[pl.ds(m * ks, ks)], ga.at[m], l_sem.at[0])
    own.start()
    own.wait()
    for d in range(1, parts):
        copy_a(d).wait()
    for d in range(1, groups):
        copy_b(d).start()
    own = pltpu.make_async_copy(
        ga.at[b // ratio, :, :, pl.ds(pl.multiple_of(lax.rem(b, ratio) * block, block), block)], gb.at[b], l_sem.at[1])
    own.start()
    own.wait()

    plane_start = starts_ref[2 * z]
    plane_end = starts_ref[2 * z + 2]
    my_end = starts_ref[b + 1]
    far = jnp.maximum(z, planes - 1 - z)

    def place(s, c):
        p = lax.rem(s, pairs)
        number = 2 * p + y
        mine = hid_ref[jnp.clip(number - my_start, 0, keep_most - 1), :, cols(c)]
        theirs = y_recv[c][jnp.clip((number - peer_start) // 2, 0, half - 1)]
        is_mine = jnp.logical_and(number >= my_start, number < my_end)
        loc[p, :, cols(c)] = jnp.where(is_mine, mine, theirs)

    def gets_dn(s):
        return jnp.logical_and(z < planes - 1, lax.rem(s, pairs) >= low(z + 1))

    def gets_up(s):
        return jnp.logical_and(z > 0, lax.rem(s, pairs) < high(z))

    def gives_dn(s):
        return jnp.logical_and(z > 0, lax.rem(s, pairs) >= low(z))

    def gives_up(s):
        return jnp.logical_and(z < planes - 1, lax.rem(s, pairs) < high(z + 1))

    @pl.loop(0, steps + LEAD * (planes - 1))
    def _(t):
        sd = t - LEAD * (planes - 1 - z)
        su = t - LEAD * z
        sf = t - LEAD * far

        for c in range(chunks):

            @pl.when(t == c * pairs)
            def _():
                @pl.loop(0, half)
                def _(k):
                    copy_y(c, k).wait()

            @pl.when(jnp.logical_and(t >= c * pairs, t < (c + 1) * pairs))
            def _():
                place(t, c)

        @pl.when(t == steps // 2)
        def _():
            for d in range(1, groups):
                copy_b(d).wait()
            for d in range(1, parts):
                copy_c(d).start()

        @pl.when(jnp.logical_and(sd >= 0, sd < steps))
        def _():
            p, c = lax.rem(sd, pairs), sd // pairs

            @pl.when(gets_dn(sd))
            def _():
                copy_dn(sd).wait_recv()

                @pl.when(z > 0)
                def _():
                    dn_send[p, :, cols(c)] = jnp.where(
                        2 * p + y >= plane_end, dn_recv[p, :, cols(c)], loc[p, :, cols(c)])
                    copy_dn(sd).start()

            @pl.when(jnp.logical_and(jnp.logical_not(gets_dn(sd)), gives_dn(sd)))
            def _():
                dn_send[p, :, cols(c)] = loc[p, :, cols(c)]
                copy_dn(sd).start()

        @pl.when(jnp.logical_and(su >= 0, su < steps))
        def _():
            p, c = lax.rem(su, pairs), su // pairs

            @pl.when(gets_up(su))
            def _():
                copy_up(su).wait_recv()

                @pl.when(z < planes - 1)
                def _():
                    up_send[p, :, cols(c)] = jnp.where(
                        2 * p + y < plane_start, up_recv[p, :, cols(c)], loc[p, :, cols(c)])
                    copy_up(su).start()

            @pl.when(jnp.logical_and(jnp.logical_not(gets_up(su)), gives_up(su)))
            def _():
                up_send[p, :, cols(c)] = loc[p, :, cols(c)]
                copy_up(su).start()

        @pl.when(jnp.logical_and(sf >= 0, sf < steps))
        def _():
            p, c = lax.rem(sf, pairs), sf // pairs
            number = 2 * p + y
            out_ref[p, y, :, cols(c)] = loc[p, :, cols(c)]

            @pl.when(gets_dn(sf))
            def _():
                out_ref[p, y, :, cols(c)] = jnp.where(
                    number >= plane_end, dn_recv[p, :, cols(c)], out_ref[p, y, :, cols(c)])

            @pl.when(gets_up(sf))
            def _():
                out_ref[p, y, :, cols(c)] = jnp.where(
                    number < plane_start, up_recv[p, :, cols(c)], out_ref[p, y, :, cols(c)])

            copy_f(sf, y).start()

    own = pltpu.make_async_copy(gb, gc.at[m], l_sem.at[2])
    own.start()
    own.wait()
    for d in range(1, parts):
        copy_c(d).wait()

    @pl.loop(0, total)
    def _(i):
        g = jnp.int32(0)
        for q in range(1, groups):
            g = g + (starts_ref[q] <= i).astype(jnp.int32)
        j = jnp.clip(i - starts_ref[g], 0, keep_most - 1)
        gout_ref[i] = gc[j // ks, g, lax.rem(j, ks)]

    @pl.loop(0, steps)
    def _(s):
        copy_f(s, y).wait_send()
        copy_f(s, 1 - y).wait_recv()

        @pl.when(gives_dn(s))
        def _():
            copy_dn(s).wait_send()

        @pl.when(gives_up(s))
        def _():
            copy_up(s).wait_send()


def exchange(count, hid, grad, groups, parts, total):
    keep_most, _, wide = hid.shape
    part = grad.shape[2]
    pairs = total // 2
    ks = keep_most // parts
    block = part * parts // groups
    bf16 = jnp.bfloat16
    chunks = 4 if wide % 512 == 0 else 1
    steps = chunks * pairs
    count = jnp.broadcast_to(count.reshape(1, 1), (1, 128))
    dma = pltpu.SemaphoreType.DMA
    chain = pltpu.VMEM((pairs, SEQ, wide), bf16)
    return pl.pallas_call(
        functools.partial(exchange_kernel, groups, parts, keep_most, total, chunks),
        out_shape=[
            jax.ShapeDtypeStruct((pairs, 2, SEQ, wide), bf16),
            jax.ShapeDtypeStruct((total, SEQ, block), bf16),
        ],
        in_specs=[
            pl.BlockSpec(memory_space=pltpu.VMEM),
            pl.BlockSpec(memory_space=pltpu.VMEM),
            pl.BlockSpec(memory_space=pltpu.VMEM),
        ],
        out_specs=[pl.BlockSpec(memory_space=pltpu.VMEM)] * 2,
        scratch_shapes=[
            pltpu.VMEM((groups, 1, 128), jnp.int32),
            pltpu.SMEM((groups, 1, 128), jnp.int32),
            pltpu.SMEM((groups + 1,), jnp.int32),
            pltpu.VMEM((keep_most // 2, SEQ, wide), bf16),
            [pltpu.VMEM((keep_most // 2, SEQ, wide // chunks), bf16)] * chunks,
            chain, chain, chain, chain, chain,
            pltpu.VMEM((parts, ks, SEQ, part), bf16),
            pltpu.VMEM((groups, ks, SEQ, block), bf16),
            pltpu.VMEM((parts, groups, ks, SEQ, block), bf16),
            dma((chunks * keep_most // 2,)), dma((chunks * keep_most // 2,)),
            dma((steps,)), dma((steps,)), dma((steps,)), dma((steps,)), dma((steps,)), dma((steps,)),
            dma((parts,)), dma((parts,)), dma((groups,)), dma((groups,)), dma((parts,)), dma((parts,)),
            dma((groups,)), dma((groups,)), dma((5,)),
        ],
        compiler_params=pltpu.CompilerParams(
            collective_id=0, has_side_effects=True, vmem_limit_bytes=60 * 1024 * 1024
        ),
    )(count, hid, grad)


def on_device(gate_act, up_act, upstream, kept_index, kept_count):
    groups, parts = lax.axis_size("batch"), lax.axis_size("mp")
    share = groups // 2
    total = groups * share
    wide, part = gate_act.shape[1], upstream.shape[1]
    hid, grad = pick(
        kept_index[0],
        gate_act.reshape(CAND, SEQ, wide),
        up_act.reshape(CAND, SEQ, wide),
        upstream.reshape(CAND, SEQ, part),
    )
    rows, columns = exchange(kept_count, hid, grad, groups, parts, total)
    summed = lax.dot_general(
        columns.reshape(total * SEQ, columns.shape[2]),
        rows.reshape(total * SEQ, wide),
        (((0,), (0,)), ((), ())),
        preferred_element_type=jnp.float32,
    )
    return (summed * (1.0 / math.sqrt(total * SEQ))).astype(jnp.bfloat16)


def solution(mesh):
    placed = (P("batch", "mp"), P("batch", "mp"), P("batch", "mp"), P("batch", None), P("batch"))
    return jax.shard_map(
        on_device, mesh=mesh, in_specs=placed, out_specs=P("batch", "mp"), check_vma=False
    )
```

```python
import functools
import math

import jax
import jax.numpy as jnp
from jax import lax
from jax.experimental import pallas as pl
from jax.experimental.pallas import tpu as pltpu
from jax.sharding import PartitionSpec as P

SEQ = 24
CAND = 32
MESH = pl.DeviceIdType.MESH
LEAD = 4


def pick_kernel(keep_most, index_ref, gate_all, up_all, grad_all, hidden_ref, grad_ref, gate, up, sems):
    def copies(j):
        at = index_ref[j]
        return (
            pltpu.make_async_copy(gate_all.at[at], gate.at[j], sems.at[0, j]),
            pltpu.make_async_copy(up_all.at[at], up.at[j], sems.at[1, j]),
            pltpu.make_async_copy(grad_all.at[at], grad_ref.at[j], sems.at[2, j]),
        )

    for j in range(keep_most):
        for copy in copies(j)[:2]:
            copy.start()
    for j in range(keep_most):
        copies(j)[2].start()

    @pl.loop(0, keep_most)
    def _(j):
        for copy in copies(j)[:2]:
            copy.wait()
        v = gate[j].astype(jnp.float32)
        hidden_ref[j] = (jax.nn.silu(v) * up[j].astype(jnp.float32)).astype(jnp.bfloat16)

    for j in range(keep_most):
        copies(j)[2].wait()


def pick(picked, gate_all, up_all, grad_all):
    keep_most = picked.shape[0]
    wide, part = gate_all.shape[2], grad_all.shape[2]
    rows = pltpu.VMEM((keep_most, SEQ, wide), jnp.bfloat16)
    return pl.pallas_call(
        functools.partial(pick_kernel, keep_most),
        in_specs=[pl.BlockSpec(memory_space=pltpu.SMEM)] + [pl.BlockSpec(memory_space=pl.ANY)] * 3,
        out_specs=[pl.BlockSpec(memory_space=pltpu.VMEM)] * 2,
        out_shape=[
            jax.ShapeDtypeStruct((keep_most, SEQ, wide), jnp.bfloat16),
            jax.ShapeDtypeStruct((keep_most, SEQ, part), jnp.bfloat16),
        ],
        scratch_shapes=[rows, rows, pltpu.SemaphoreType.DMA((3, keep_most))],
    )(picked, gate_all, up_all, grad_all)


def exchange_kernel(
    groups, parts, keep_most, total, chunks,
    count_ref, hid_ref, grad_ref, out_ref, gout_ref,
    counts_in, counts_ref, starts_ref,
    y_send, y_recv, fin, loc, dn_recv, dn_send, up_recv, up_send, ga, gb, gc,
    ys_sem, yr_sem, dns_sem, dnr_sem, ups_sem, upr_sem, fs_sem, fr_sem,
    as_sem, ar_sem, bs_sem, br_sem, cs_sem, cr_sem, ns_sem, nr_sem, o_sem, l_sem,
):
    b, m = lax.axis_index("batch"), lax.axis_index("mp")
    planes, pairs = groups // 2, total // 2
    z, y = b // 2, lax.rem(b, 2)
    peer = z * 2 + 1 - y
    ks = keep_most // parts
    ratio = groups // parts
    block = grad_ref.shape[2] // ratio
    width = hid_ref.shape[2] // chunks
    half = keep_most // 2
    steps = chunks * pairs

    def cols(c):
        if isinstance(c, int):
            return pl.ds(c * width, width)
        return pl.ds(pl.multiple_of(c * width, width), width)

    def low(plane):
        return jnp.maximum(2 * plane, total - 2 * keep_most * (planes - plane)) // 2

    def high(plane):
        return (jnp.minimum(2 * keep_most * plane, total - 2 * (planes - plane)) + 1) // 2

    barrier = pltpu.get_barrier_semaphore()
    for d in range(1, groups):
        pl.semaphore_signal(barrier, inc=1, device_id=(lax.rem(b + d, groups), m), device_id_type=MESH)
    for d in range(1, parts):
        pl.semaphore_signal(barrier, inc=1, device_id=(b, lax.rem(m + d, parts)), device_id_type=MESH)
    pl.semaphore_wait(barrier, groups + parts - 2)

    def copy_a(d):
        other = lax.rem(m + d, parts)
        return pltpu.make_async_remote_copy(
            src_ref=grad_ref.at[pl.ds(other * ks, ks)], dst_ref=ga.at[m],
            send_sem=as_sem.at[d], recv_sem=ar_sem.at[d],
            device_id=(b, other), device_id_type=MESH)

    def copy_b(d):
        other = lax.rem(b + d, groups)
        return pltpu.make_async_remote_copy(
            src_ref=ga.at[other // ratio, :, :, pl.ds(pl.multiple_of(lax.rem(other, ratio) * block, block), block)],
            dst_ref=gb.at[b],
            send_sem=bs_sem.at[d], recv_sem=br_sem.at[d],
            device_id=(other, m), device_id_type=MESH)

    def copy_c(d):
        other = lax.rem(m + d, parts)
        return pltpu.make_async_remote_copy(
            src_ref=gb, dst_ref=gc.at[m],
            send_sem=cs_sem.at[d], recv_sem=cr_sem.at[d],
            device_id=(b, other), device_id_type=MESH)

    def copy_n(d):
        return pltpu.make_async_remote_copy(
            src_ref=count_ref, dst_ref=counts_in.at[b],
            send_sem=ns_sem.at[d], recv_sem=nr_sem.at[d],
            device_id=(lax.rem(b + d, groups), m), device_id_type=MESH)

    def copy_y(c, k):
        return pltpu.make_async_remote_copy(
            src_ref=y_send.at[k, :, cols(c)], dst_ref=y_recv[c].at[k],
            send_sem=ys_sem.at[c * half + k], recv_sem=yr_sem.at[c * half + k],
            device_id=(peer, m), device_id_type=MESH)

    def copy_dn(s):
        p, c = lax.rem(s, pairs), s // pairs
        return pltpu.make_async_remote_copy(
            src_ref=dn_send.at[p, :, cols(c)], dst_ref=dn_recv.at[p, :, cols(c)],
            send_sem=dns_sem.at[s], recv_sem=dnr_sem.at[s],
            device_id=(lax.rem(b + groups - 2, groups), m), device_id_type=MESH)

    def copy_up(s):
        p, c = lax.rem(s, pairs), s // pairs
        return pltpu.make_async_remote_copy(
            src_ref=up_send.at[p, :, cols(c)], dst_ref=up_recv.at[p, :, cols(c)],
            send_sem=ups_sem.at[s], recv_sem=upr_sem.at[s],
            device_id=(lax.rem(b + 2, groups), m), device_id_type=MESH)

    def copy_f(s, side):
        p, c = lax.rem(s, pairs), s // pairs
        return pltpu.make_async_remote_copy(
            src_ref=fin.at[p, :, cols(c)], dst_ref=out_ref.at[p, side, :, cols(c)],
            send_sem=fs_sem.at[s], recv_sem=fr_sem.at[s],
            device_id=(peer, m), device_id_type=MESH)

    def copy_o(s):
        p, c = lax.rem(s, pairs), s // pairs
        return pltpu.make_async_copy(fin.at[p, :, cols(c)], out_ref.at[p, y, :, cols(c)], o_sem.at[s])

    for d in range(1, groups):
        copy_n(d).start()
    own = pltpu.make_async_copy(count_ref, counts_in.at[b], l_sem.at[3])
    own.start()
    for d in range(1, parts):
        copy_a(d).start()

    own.wait()
    for d in range(1, groups):
        copy_n(d).wait()
    to_scalars = pltpu.make_async_copy(counts_in, counts_ref, l_sem.at[4])
    to_scalars.start()
    to_scalars.wait()
    before = jnp.int32(0)
    for g in range(groups):
        starts_ref[g] = before
        before = before + counts_ref[g, 0, 0]
    starts_ref[groups] = before

    my_start, peer_start = starts_ref[b], starts_ref[peer]
    offset = lax.rem(1 - y + my_start, 2)

    @pl.loop(0, half)
    def _(k):
        y_send[k] = hid_ref[2 * k + offset]
        copy_y(0, k).start()

    for c in range(1, chunks):

        @pl.loop(0, half)
        def _(k):
            copy_y(c, k).start()

    own = pltpu.make_async_copy(grad_ref.at[pl.ds(m * ks, ks)], ga.at[m], l_sem.at[0])
    own.start()
    own.wait()
    for d in range(1, parts):
        copy_a(d).wait()
    for d in range(1, groups):
        copy_b(d).start()
    own = pltpu.make_async_copy(
        ga.at[b // ratio, :, :, pl.ds(pl.multiple_of(lax.rem(b, ratio) * block, block), block)], gb.at[b], l_sem.at[1])
    own.start()
    own.wait()

    plane_start = starts_ref[2 * z]
    plane_end = starts_ref[2 * z + 2]
    my_end = starts_ref[b + 1]
    far = jnp.maximum(z, planes - 1 - z)

    def place(s, c):
        p = lax.rem(s, pairs)
        number = 2 * p + y
        mine = hid_ref[jnp.clip(number - my_start, 0, keep_most - 1), :, cols(c)]
        theirs = y_recv[c][jnp.clip((number - peer_start) // 2, 0, half - 1)]
        is_mine = jnp.logical_and(number >= my_start, number < my_end)
        loc[p, :, cols(c)] = jnp.where(is_mine, mine, theirs)

    def gets_dn(s):
        return jnp.logical_and(z < planes - 1, lax.rem(s, pairs) >= low(z + 1))

    def gets_up(s):
        return jnp.logical_and(z > 0, lax.rem(s, pairs) < high(z))

    def gives_dn(s):
        return jnp.logical_and(z > 0, lax.rem(s, pairs) >= low(z))

    def gives_up(s):
        return jnp.logical_and(z < planes - 1, lax.rem(s, pairs) < high(z + 1))

    @pl.loop(0, steps + LEAD * (planes - 1))
    def _(t):
        sd = t - LEAD * (planes - 1 - z)
        su = t - LEAD * z
        sf = t - LEAD * far

        for c in range(chunks):

            @pl.when(t == c * pairs)
            def _():
                @pl.loop(0, half)
                def _(k):
                    copy_y(c, k).wait()

            @pl.when(jnp.logical_and(t >= c * pairs, t < (c + 1) * pairs))
            def _():
                place(t, c)

        @pl.when(t == steps // 2)
        def _():
            for d in range(1, groups):
                copy_b(d).wait()
            for d in range(1, parts):
                copy_c(d).start()

        @pl.when(jnp.logical_and(sd >= 0, sd < steps))
        def _():
            p, c = lax.rem(sd, pairs), sd // pairs

            @pl.when(gets_dn(sd))
            def _():
                copy_dn(sd).wait_recv()

                @pl.when(z > 0)
                def _():
                    dn_send[p, :, cols(c)] = jnp.where(
                        2 * p + y >= plane_end, dn_recv[p, :, cols(c)], loc[p, :, cols(c)])
                    copy_dn(sd).start()

            @pl.when(jnp.logical_and(jnp.logical_not(gets_dn(sd)), gives_dn(sd)))
            def _():
                dn_send[p, :, cols(c)] = loc[p, :, cols(c)]
                copy_dn(sd).start()

        @pl.when(jnp.logical_and(su >= 0, su < steps))
        def _():
            p, c = lax.rem(su, pairs), su // pairs

            @pl.when(gets_up(su))
            def _():
                copy_up(su).wait_recv()

                @pl.when(z < planes - 1)
                def _():
                    up_send[p, :, cols(c)] = jnp.where(
                        2 * p + y < plane_start, up_recv[p, :, cols(c)], loc[p, :, cols(c)])
                    copy_up(su).start()

            @pl.when(jnp.logical_and(jnp.logical_not(gets_up(su)), gives_up(su)))
            def _():
                up_send[p, :, cols(c)] = loc[p, :, cols(c)]
                copy_up(su).start()

        @pl.when(jnp.logical_and(sf >= 0, sf < steps))
        def _():
            p, c = lax.rem(sf, pairs), sf // pairs
            number = 2 * p + y
            fin[p, :, cols(c)] = loc[p, :, cols(c)]

            @pl.when(gets_dn(sf))
            def _():
                fin[p, :, cols(c)] = jnp.where(
                    number >= plane_end, dn_recv[p, :, cols(c)], fin[p, :, cols(c)])

            @pl.when(gets_up(sf))
            def _():
                fin[p, :, cols(c)] = jnp.where(
                    number < plane_start, up_recv[p, :, cols(c)], fin[p, :, cols(c)])

            copy_f(sf, y).start()
            copy_o(sf).start()

    own = pltpu.make_async_copy(gb, gc.at[m], l_sem.at[2])
    own.start()
    own.wait()
    for d in range(1, parts):
        copy_c(d).wait()

    @pl.loop(0, total)
    def _(i):
        g = jnp.int32(0)
        for q in range(1, groups):
            g = g + (starts_ref[q] <= i).astype(jnp.int32)
        j = jnp.clip(i - starts_ref[g], 0, keep_most - 1)
        gout_ref[i] = gc[j // ks, g, lax.rem(j, ks)]

    @pl.loop(0, steps)
    def _(s):
        copy_f(s, y).wait_send()
        copy_o(s).wait()
        copy_f(s, 1 - y).wait_recv()

        @pl.when(gives_dn(s))
        def _():
            copy_dn(s).wait_send()

        @pl.when(gives_up(s))
        def _():
            copy_up(s).wait_send()


def exchange(count, hid, grad, groups, parts, total):
    keep_most, _, wide = hid.shape
    part = grad.shape[2]
    pairs = total // 2
    ks = keep_most // parts
    block = part * parts // groups
    bf16 = jnp.bfloat16
    chunks = 4 if wide % 512 == 0 else 1
    steps = chunks * pairs
    count = jnp.broadcast_to(count.reshape(1, 1), (1, 128))
    dma = pltpu.SemaphoreType.DMA
    chain = pltpu.VMEM((pairs, SEQ, wide), bf16)
    return pl.pallas_call(
        functools.partial(exchange_kernel, groups, parts, keep_most, total, chunks),
        out_shape=[
            jax.ShapeDtypeStruct((pairs, 2, SEQ, wide), bf16),
            jax.ShapeDtypeStruct((total, SEQ, block), bf16),
        ],
        in_specs=[
            pl.BlockSpec(memory_space=pltpu.VMEM),
            pl.BlockSpec(memory_space=pltpu.VMEM),
            pl.BlockSpec(memory_space=pltpu.VMEM),
        ],
        out_specs=[pl.BlockSpec(memory_space=pl.ANY), pl.BlockSpec(memory_space=pltpu.VMEM)],
        scratch_shapes=[
            pltpu.VMEM((groups, 1, 128), jnp.int32),
            pltpu.SMEM((groups, 1, 128), jnp.int32),
            pltpu.SMEM((groups + 1,), jnp.int32),
            pltpu.VMEM((keep_most // 2, SEQ, wide), bf16),
            [pltpu.VMEM((keep_most // 2, SEQ, wide // chunks), bf16)] * chunks,
            chain, chain, chain, chain, chain, chain,
            pltpu.VMEM((parts, ks, SEQ, part), bf16),
            pltpu.VMEM((groups, ks, SEQ, block), bf16),
            pltpu.VMEM((parts, groups, ks, SEQ, block), bf16),
            dma((chunks * keep_most // 2,)), dma((chunks * keep_most // 2,)),
            dma((steps,)), dma((steps,)), dma((steps,)), dma((steps,)), dma((steps,)), dma((steps,)),
            dma((parts,)), dma((parts,)), dma((groups,)), dma((groups,)), dma((parts,)), dma((parts,)),
            dma((groups,)), dma((groups,)), dma((steps,)), dma((5,)),
        ],
        compiler_params=pltpu.CompilerParams(
            collective_id=0, has_side_effects=True, vmem_limit_bytes=60 * 1024 * 1024
        ),
    )(count, hid, grad)


def on_device(gate_act, up_act, upstream, kept_index, kept_count):
    groups, parts = lax.axis_size("batch"), lax.axis_size("mp")
    share = groups // 2
    total = groups * share
    wide, part = gate_act.shape[1], upstream.shape[1]
    hid, grad = pick(
        kept_index[0],
        gate_act.reshape(CAND, SEQ, wide),
        up_act.reshape(CAND, SEQ, wide),
        upstream.reshape(CAND, SEQ, part),
    )
    rows, columns = exchange(kept_count, hid, grad, groups, parts, total)
    summed = lax.dot_general(
        columns.reshape(total * SEQ, columns.shape[2]),
        rows.reshape(total * SEQ, wide),
        (((0,), (0,)), ((), ())),
        preferred_element_type=jnp.float32,
    )
    return (summed * (1.0 / math.sqrt(total * SEQ))).astype(jnp.bfloat16)


def solution(mesh):
    placed = (P("batch", "mp"), P("batch", "mp"), P("batch", "mp"), P("batch", None), P("batch"))
    return jax.shard_map(
        on_device, mesh=mesh, in_specs=placed, out_specs=P("batch", "mp"), check_vma=False
    )
```

```python
import functools
import math

import jax
import jax.numpy as jnp
from jax import lax
from jax.experimental import pallas as pl
from jax.experimental.pallas import tpu as pltpu
from jax.sharding import PartitionSpec as P

SEQ = 24
CAND = 32
MESH = pl.DeviceIdType.MESH
LEAD = 6


def pick_kernel(keep_most, index_ref, gate_all, up_all, grad_all, hidden_ref, grad_ref, gate, up, sems):
    def copies(j):
        at = index_ref[j]
        return (
            pltpu.make_async_copy(gate_all.at[at], gate.at[j], sems.at[0, j]),
            pltpu.make_async_copy(up_all.at[at], up.at[j], sems.at[1, j]),
            pltpu.make_async_copy(grad_all.at[at], grad_ref.at[j], sems.at[2, j]),
        )

    for j in range(keep_most):
        for copy in copies(j)[:2]:
            copy.start()
    for j in range(keep_most):
        copies(j)[2].start()

    @pl.loop(0, keep_most)
    def _(j):
        for copy in copies(j)[:2]:
            copy.wait()
        v = gate[j].astype(jnp.float32)
        hidden_ref[j] = (jax.nn.silu(v) * up[j].astype(jnp.float32)).astype(jnp.bfloat16)

    for j in range(keep_most):
        copies(j)[2].wait()


def pick(picked, gate_all, up_all, grad_all):
    keep_most = picked.shape[0]
    wide, part = gate_all.shape[2], grad_all.shape[2]
    rows = pltpu.VMEM((keep_most, SEQ, wide), jnp.bfloat16)
    return pl.pallas_call(
        functools.partial(pick_kernel, keep_most),
        in_specs=[pl.BlockSpec(memory_space=pltpu.SMEM)] + [pl.BlockSpec(memory_space=pl.ANY)] * 3,
        out_specs=[pl.BlockSpec(memory_space=pltpu.VMEM)] * 2,
        out_shape=[
            jax.ShapeDtypeStruct((keep_most, SEQ, wide), jnp.bfloat16),
            jax.ShapeDtypeStruct((keep_most, SEQ, part), jnp.bfloat16),
        ],
        scratch_shapes=[rows, rows, pltpu.SemaphoreType.DMA((3, keep_most))],
    )(picked, gate_all, up_all, grad_all)


def exchange_kernel(
    groups, parts, keep_most, total, chunks,
    count_ref, hid_ref, grad_ref, out_ref, gout_ref,
    counts_in, counts_ref, starts_ref,
    y_send, y_recv, fin, loc, dn_recv, dn_send, up_recv, up_send, ga, gb, gc,
    ys_sem, yr_sem, dns_sem, dnr_sem, ups_sem, upr_sem, fs_sem, fr_sem,
    as_sem, ar_sem, bs_sem, br_sem, cs_sem, cr_sem, ns_sem, nr_sem, o_sem, l_sem,
):
    b, m = lax.axis_index("batch"), lax.axis_index("mp")
    planes, pairs = groups // 2, total // 2
    z, y = b // 2, lax.rem(b, 2)
    peer = z * 2 + 1 - y
    ks = keep_most // parts
    ratio = groups // parts
    block = grad_ref.shape[2] // ratio
    width = hid_ref.shape[2] // chunks
    half = keep_most // 2
    steps = chunks * pairs

    def cols(c):
        if isinstance(c, int):
            return pl.ds(c * width, width)
        return pl.ds(pl.multiple_of(c * width, width), width)

    def low(plane):
        return jnp.maximum(2 * plane, total - 2 * keep_most * (planes - plane)) // 2

    def high(plane):
        return (jnp.minimum(2 * keep_most * plane, total - 2 * (planes - plane)) + 1) // 2

    barrier = pltpu.get_barrier_semaphore()
    for d in range(1, groups):
        pl.semaphore_signal(barrier, inc=1, device_id=(lax.rem(b + d, groups), m), device_id_type=MESH)
    for d in range(1, parts):
        pl.semaphore_signal(barrier, inc=1, device_id=(b, lax.rem(m + d, parts)), device_id_type=MESH)
    pl.semaphore_wait(barrier, groups + parts - 2)

    def copy_a(d):
        other = lax.rem(m + d, parts)
        return pltpu.make_async_remote_copy(
            src_ref=grad_ref.at[pl.ds(other * ks, ks)], dst_ref=ga.at[m],
            send_sem=as_sem.at[d], recv_sem=ar_sem.at[d],
            device_id=(b, other), device_id_type=MESH)

    def copy_b(d):
        other = lax.rem(b + d, groups)
        return pltpu.make_async_remote_copy(
            src_ref=ga.at[other // ratio, :, :, pl.ds(pl.multiple_of(lax.rem(other, ratio) * block, block), block)],
            dst_ref=gb.at[b],
            send_sem=bs_sem.at[d], recv_sem=br_sem.at[d],
            device_id=(other, m), device_id_type=MESH)

    def copy_c(d):
        other = lax.rem(m + d, parts)
        return pltpu.make_async_remote_copy(
            src_ref=gb, dst_ref=gc.at[m],
            send_sem=cs_sem.at[d], recv_sem=cr_sem.at[d],
            device_id=(b, other), device_id_type=MESH)

    def copy_n(d):
        return pltpu.make_async_remote_copy(
            src_ref=count_ref, dst_ref=counts_in.at[b],
            send_sem=ns_sem.at[d], recv_sem=nr_sem.at[d],
            device_id=(lax.rem(b + d, groups), m), device_id_type=MESH)

    def copy_y(c, k):
        return pltpu.make_async_remote_copy(
            src_ref=y_send.at[k, :, cols(c)], dst_ref=y_recv[c].at[k],
            send_sem=ys_sem.at[c * half + k], recv_sem=yr_sem.at[c * half + k],
            device_id=(peer, m), device_id_type=MESH)

    def copy_dn(s):
        p, c = lax.rem(s, pairs), s // pairs
        return pltpu.make_async_remote_copy(
            src_ref=dn_send.at[p, :, cols(c)], dst_ref=dn_recv.at[p, :, cols(c)],
            send_sem=dns_sem.at[s], recv_sem=dnr_sem.at[s],
            device_id=(lax.rem(b + groups - 2, groups), m), device_id_type=MESH)

    def copy_up(s):
        p, c = lax.rem(s, pairs), s // pairs
        return pltpu.make_async_remote_copy(
            src_ref=up_send.at[p, :, cols(c)], dst_ref=up_recv.at[p, :, cols(c)],
            send_sem=ups_sem.at[s], recv_sem=upr_sem.at[s],
            device_id=(lax.rem(b + 2, groups), m), device_id_type=MESH)

    def copy_f(s, side):
        p, c = lax.rem(s, pairs), s // pairs
        return pltpu.make_async_remote_copy(
            src_ref=fin.at[p, :, cols(c)], dst_ref=out_ref.at[p, side, :, cols(c)],
            send_sem=fs_sem.at[s], recv_sem=fr_sem.at[s],
            device_id=(peer, m), device_id_type=MESH)

    def copy_o(s):
        p, c = lax.rem(s, pairs), s // pairs
        return pltpu.make_async_copy(fin.at[p, :, cols(c)], out_ref.at[p, y, :, cols(c)], o_sem.at[s])

    for d in range(1, groups):
        copy_n(d).start()
    own = pltpu.make_async_copy(count_ref, counts_in.at[b], l_sem.at[3])
    own.start()
    for d in range(1, parts):
        copy_a(d).start()

    own.wait()
    for d in range(1, groups):
        copy_n(d).wait()
    to_scalars = pltpu.make_async_copy(counts_in, counts_ref, l_sem.at[4])
    to_scalars.start()
    to_scalars.wait()
    before = jnp.int32(0)
    for g in range(groups):
        starts_ref[g] = before
        before = before + counts_ref[g, 0, 0]
    starts_ref[groups] = before

    my_start, peer_start = starts_ref[b], starts_ref[peer]
    offset = lax.rem(1 - y + my_start, 2)

    @pl.loop(0, half)
    def _(k):
        y_send[k] = hid_ref[2 * k + offset]
        copy_y(0, k).start()

    for c in range(1, chunks):

        @pl.loop(0, half)
        def _(k):
            copy_y(c, k).start()

    own = pltpu.make_async_copy(grad_ref.at[pl.ds(m * ks, ks)], ga.at[m], l_sem.at[0])
    own.start()
    own.wait()
    for d in range(1, parts):
        copy_a(d).wait()
    for d in range(1, groups):
        copy_b(d).start()
    own = pltpu.make_async_copy(
        ga.at[b // ratio, :, :, pl.ds(pl.multiple_of(lax.rem(b, ratio) * block, block), block)], gb.at[b], l_sem.at[1])
    own.start()
    own.wait()

    plane_start = starts_ref[2 * z]
    plane_end = starts_ref[2 * z + 2]
    my_end = starts_ref[b + 1]
    far = jnp.maximum(z, planes - 1 - z)

    def place(s, c):
        p = lax.rem(s, pairs)
        number = 2 * p + y
        mine = hid_ref[jnp.clip(number - my_start, 0, keep_most - 1), :, cols(c)]
        theirs = y_recv[c][jnp.clip((number - peer_start) // 2, 0, half - 1)]
        is_mine = jnp.logical_and(number >= my_start, number < my_end)
        loc[p, :, cols(c)] = jnp.where(is_mine, mine, theirs)

    def gets_dn(s):
        return jnp.logical_and(z < planes - 1, lax.rem(s, pairs) >= low(z + 1))

    def gets_up(s):
        return jnp.logical_and(z > 0, lax.rem(s, pairs) < high(z))

    def gives_dn(s):
        return jnp.logical_and(z > 0, lax.rem(s, pairs) >= low(z))

    def gives_up(s):
        return jnp.logical_and(z < planes - 1, lax.rem(s, pairs) < high(z + 1))

    @pl.loop(0, steps + LEAD * (planes - 1))
    def _(t):
        sd = t - LEAD * (planes - 1 - z)
        su = t - LEAD * z
        sf = t - LEAD * far

        for c in range(chunks):

            @pl.when(t == c * pairs)
            def _():
                @pl.loop(0, half)
                def _(k):
                    copy_y(c, k).wait()

            @pl.when(jnp.logical_and(t >= c * pairs, t < (c + 1) * pairs))
            def _():
                place(t, c)

        @pl.when(t == steps // 3)
        def _():
            for d in range(1, groups):
                copy_b(d).wait()
            for d in range(1, parts):
                copy_c(d).start()

        @pl.when(jnp.logical_and(sd >= 0, sd < steps))
        def _():
            p, c = lax.rem(sd, pairs), sd // pairs

            @pl.when(gets_dn(sd))
            def _():
                copy_dn(sd).wait_recv()

                @pl.when(z > 0)
                def _():
                    dn_send[p, :, cols(c)] = jnp.where(
                        2 * p + y >= plane_end, dn_recv[p, :, cols(c)], loc[p, :, cols(c)])
                    copy_dn(sd).start()

            @pl.when(jnp.logical_and(jnp.logical_not(gets_dn(sd)), gives_dn(sd)))
            def _():
                dn_send[p, :, cols(c)] = loc[p, :, cols(c)]
                copy_dn(sd).start()

        @pl.when(jnp.logical_and(su >= 0, su < steps))
        def _():
            p, c = lax.rem(su, pairs), su // pairs

            @pl.when(gets_up(su))
            def _():
                copy_up(su).wait_recv()

                @pl.when(z < planes - 1)
                def _():
                    up_send[p, :, cols(c)] = jnp.where(
                        2 * p + y < plane_start, up_recv[p, :, cols(c)], loc[p, :, cols(c)])
                    copy_up(su).start()

            @pl.when(jnp.logical_and(jnp.logical_not(gets_up(su)), gives_up(su)))
            def _():
                up_send[p, :, cols(c)] = loc[p, :, cols(c)]
                copy_up(su).start()

        @pl.when(jnp.logical_and(sf >= 0, sf < steps))
        def _():
            p, c = lax.rem(sf, pairs), sf // pairs
            number = 2 * p + y
            fin[p, :, cols(c)] = loc[p, :, cols(c)]

            @pl.when(gets_dn(sf))
            def _():
                fin[p, :, cols(c)] = jnp.where(
                    number >= plane_end, dn_recv[p, :, cols(c)], fin[p, :, cols(c)])

            @pl.when(gets_up(sf))
            def _():
                fin[p, :, cols(c)] = jnp.where(
                    number < plane_start, up_recv[p, :, cols(c)], fin[p, :, cols(c)])

            copy_f(sf, y).start()
            copy_o(sf).start()

    own = pltpu.make_async_copy(gb, gc.at[m], l_sem.at[2])
    own.start()
    own.wait()
    for d in range(1, parts):
        copy_c(d).wait()

    @pl.loop(0, total)
    def _(i):
        g = jnp.int32(0)
        for q in range(1, groups):
            g = g + (starts_ref[q] <= i).astype(jnp.int32)
        j = jnp.clip(i - starts_ref[g], 0, keep_most - 1)
        gout_ref[i] = gc[j // ks, g, lax.rem(j, ks)]

    @pl.loop(0, steps)
    def _(s):
        copy_f(s, y).wait_send()
        copy_o(s).wait()
        copy_f(s, 1 - y).wait_recv()

        @pl.when(gives_dn(s))
        def _():
            copy_dn(s).wait_send()

        @pl.when(gives_up(s))
        def _():
            copy_up(s).wait_send()


def exchange(count, hid, grad, groups, parts, total):
    keep_most, _, wide = hid.shape
    part = grad.shape[2]
    pairs = total // 2
    ks = keep_most // parts
    block = part * parts // groups
    bf16 = jnp.bfloat16
    chunks = 4 if wide % 512 == 0 else 1
    steps = chunks * pairs
    count = jnp.broadcast_to(count.reshape(1, 1), (1, 128))
    dma = pltpu.SemaphoreType.DMA
    chain = pltpu.VMEM((pairs, SEQ, wide), bf16)
    return pl.pallas_call(
        functools.partial(exchange_kernel, groups, parts, keep_most, total, chunks),
        out_shape=[
            jax.ShapeDtypeStruct((pairs, 2, SEQ, wide), bf16),
            jax.ShapeDtypeStruct((total, SEQ, block), bf16),
        ],
        in_specs=[
            pl.BlockSpec(memory_space=pltpu.VMEM),
            pl.BlockSpec(memory_space=pltpu.VMEM),
            pl.BlockSpec(memory_space=pltpu.VMEM),
        ],
        out_specs=[pl.BlockSpec(memory_space=pl.ANY), pl.BlockSpec(memory_space=pltpu.VMEM)],
        scratch_shapes=[
            pltpu.VMEM((groups, 1, 128), jnp.int32),
            pltpu.SMEM((groups, 1, 128), jnp.int32),
            pltpu.SMEM((groups + 1,), jnp.int32),
            pltpu.VMEM((keep_most // 2, SEQ, wide), bf16),
            [pltpu.VMEM((keep_most // 2, SEQ, wide // chunks), bf16)] * chunks,
            chain, chain, chain, chain, chain, chain,
            pltpu.VMEM((parts, ks, SEQ, part), bf16),
            pltpu.VMEM((groups, ks, SEQ, block), bf16),
            pltpu.VMEM((parts, groups, ks, SEQ, block), bf16),
            dma((chunks * keep_most // 2,)), dma((chunks * keep_most // 2,)),
            dma((steps,)), dma((steps,)), dma((steps,)), dma((steps,)), dma((steps,)), dma((steps,)),
            dma((parts,)), dma((parts,)), dma((groups,)), dma((groups,)), dma((parts,)), dma((parts,)),
            dma((groups,)), dma((groups,)), dma((steps,)), dma((5,)),
        ],
        compiler_params=pltpu.CompilerParams(
            collective_id=0, has_side_effects=True, vmem_limit_bytes=60 * 1024 * 1024
        ),
    )(count, hid, grad)


def on_device(gate_act, up_act, upstream, kept_index, kept_count):
    groups, parts = lax.axis_size("batch"), lax.axis_size("mp")
    share = groups // 2
    total = groups * share
    wide, part = gate_act.shape[1], upstream.shape[1]
    hid, grad = pick(
        kept_index[0],
        gate_act.reshape(CAND, SEQ, wide),
        up_act.reshape(CAND, SEQ, wide),
        upstream.reshape(CAND, SEQ, part),
    )
    rows, columns = exchange(kept_count, hid, grad, groups, parts, total)
    summed = lax.dot_general(
        columns.reshape(total * SEQ, columns.shape[2]),
        rows.reshape(total * SEQ, wide),
        (((0,), (0,)), ((), ())),
        preferred_element_type=jnp.float32,
    )
    return (summed * (1.0 / math.sqrt(total * SEQ))).astype(jnp.bfloat16)


def solution(mesh):
    placed = (P("batch", "mp"), P("batch", "mp"), P("batch", "mp"), P("batch", None), P("batch"))
    return jax.shard_map(
        on_device, mesh=mesh, in_specs=placed, out_specs=P("batch", "mp"), check_vma=False
    )
```
